256 devices in a mesh: leaf: 8 (over z), trunk: 32 (over y, x, core).
Axes of the slice: x: 4, y: 4, z: 8, core: 2. Of those that a mesh axis runs over, the one named last changes fastest.
Arguments:
- trunk_tokens: bfloat16 [16, 8192, 1024], P('leaf', 'trunk'), may hold values from -6 to 6
- branch_tokens: bfloat16 [2048, 128, 1024], P(('leaf', 'trunk')), may hold values from -6 to 6
- fork_offset: int32 [8, 32, 8], P('leaf', 'trunk'), may hold values from 0 to 255
- fork_tree: int32 [8, 32, 8], P('leaf', 'trunk'), may hold values from 0 to 1
- branch_len: int32 [2048], P(('leaf', 'trunk')), may hold values from 0 to 128, as said below
- w_query: bfloat16 [1024, 1024], P('trunk'), may hold values from -0.1875 to 0.1875
- w_key: bfloat16 [1024, 1024], P('trunk'), may hold values from -0.1875 to 0.1875
- w_value: bfloat16 [1024, 1024], P('trunk'), may hold values from -0.1875 to 0.1875
- w_out: bfloat16 [1024, 1024], P('trunk'), may hold values from -0.1875 to 0.1875
Outputs:
- mixed: bfloat16 [2048, 128, 1024], P(('leaf', 'trunk'))
The draws below stay inside these ranges and needn't reach their ends.
Inputs may be any that keep to these rules, and one draw needn't show every extreme that they name: `branch_len`: each length is a multiple of 128; some slot has the full 128 in every draw.
All inputs are finite; a program needn't handle non-finite values.
Results may differ from the reference program's by a relative error of at most 0.0065.
Values may be sent and summed in bfloat16 or wider, within the bound.
A program may use at most 128 MiB of HBM per device.

```python
import jax
import jax.numpy as jnp
from jax import lax

D = 1024
H = 8
DH = 128
HD = 1024
TRUNK_TOK = 256
TREES_DEV = 2
CAP = 1
BLEN = 128
SLOTS = 8
TREES = 16
TRUNK_LEN = 8192
BRANCHES = 2048
N_LEAF = 8
N_TRUNK = 32


def draw_branch_len(key, part):
    key_keep = jax.random.fold_in(key, 11)
    key_size = jax.random.fold_in(key, 23)
    keep = jax.random.randint(key_keep, (BRANCHES,), 0, 4) > 0
    sizes = 128 * jax.random.randint(key_size, (BRANCHES,), 1, BLEN // 128 + 1)
    lengths = jnp.where(keep, sizes, 0)
    return lengths.at[0].set(BLEN).astype(jnp.int32)


def with_ends(values, key, low, top_value):
    dims = values.shape
    spot = [jax.random.randint(jax.random.fold_in(key, axis), (), 0, dims[axis]) for axis in range(len(dims))]
    values = values.at[tuple(spot)].set(low)
    longest = dims.index(max(dims))
    spot[longest] = (spot[longest] + 1) % dims[longest]
    return values.at[tuple(spot)].set(top_value)


def steps_of(key, shape, split, smallest, largest):
    def one(dim, blocks):
        steps = jax.random.uniform(jax.random.fold_in(jax.random.fold_in(key, 6), dim), (blocks,), jnp.float32, smallest / len(split), largest / len(split))
        return jnp.repeat(jnp.exp(steps), shape[dim] // blocks).reshape((-1,) + (1,) * (len(shape) - dim - 1))

    factor_of = one(*split[0])
    for cut in split[1:]:
        factor_of = factor_of * one(*cut)
    return factor_of


def gaussian(rng, shape, deviation, most, split=(), kind=jnp.bfloat16):
    gain = steps_of(rng, shape, split, -0.22, 0.18) if split else 1.0
    values = jax.random.normal(rng, shape, jnp.float32) * deviation * gain
    return jnp.minimum(jnp.maximum(values, -most), most).astype(kind)


def setup_inputs(seed: int = 0) -> dict:
    seeds = jax.random.split(jax.random.key(seed), 10)
    trunk_tokens = gaussian(seeds[0], (TREES, TRUNK_LEN, D), 1.0, 6.0, ((0, 8), (1, 32)))
    branch_tokens = gaussian(seeds[1], (BRANCHES, BLEN, D), 1.0, 6.0, ((0, 256),))
    fork_offset = with_ends(jax.random.randint(seeds[2], (N_LEAF, N_TRUNK, SLOTS), 0, TRUNK_TOK), jax.random.fold_in(seeds[2], 1), 0, TRUNK_TOK - 1).astype(jnp.int32)
    fork_tree = with_ends(jax.random.randint(seeds[3], (N_LEAF, N_TRUNK, SLOTS), 0, TREES_DEV), jax.random.fold_in(seeds[3], 1), 0, TREES_DEV - 1).astype(jnp.int32)
    branch_len = draw_branch_len(jax.random.fold_in(seeds[9], 71), 0)
    w_query = gaussian(seeds[5], (D, HD), D ** -0.5, 0.1875, ((0, 32),))
    w_key = gaussian(seeds[6], (D, HD), D ** -0.5, 0.1875, ((0, 32),))
    w_value = gaussian(seeds[7], (D, HD), D ** -0.5, 0.1875, ((0, 32),))
    w_out = gaussian(seeds[8], (HD, D), HD ** -0.5, 0.1875, ((0, 32),))
    return dict(trunk_tokens=trunk_tokens, branch_tokens=branch_tokens, fork_offset=fork_offset, fork_tree=fork_tree, branch_len=branch_len, w_query=w_query, w_key=w_key, w_value=w_value, w_out=w_out)


def tree_states(tokens, w_key, w_value):
    keys = jnp.dot(tokens, w_key, preferred_element_type=jnp.float32).astype(jnp.bfloat16)
    values = jnp.dot(tokens, w_value, preferred_element_type=jnp.float32).astype(jnp.bfloat16)
    key_four = keys.reshape(N_TRUNK, TRUNK_TOK, H, DH).astype(jnp.float32)
    value_four = values.reshape(N_TRUNK, TRUNK_TOK, H, DH).astype(jnp.float32)
    totals = jnp.einsum('sthd,sthf->shdf', key_four, value_four)
    prefix = jnp.cumsum(totals, axis=0) - totals
    return (keys, values, prefix)

def branch_output(tokens, state, live_len, w_query, w_key, w_value, w_out):
    query = jnp.dot(tokens, w_query, preferred_element_type=jnp.float32).astype(jnp.bfloat16)
    key = jnp.dot(tokens, w_key, preferred_element_type=jnp.float32).astype(jnp.bfloat16)
    value = jnp.dot(tokens, w_value, preferred_element_type=jnp.float32).astype(jnp.bfloat16)
    query = query.reshape(BLEN, H, DH).astype(jnp.float32)
    key = key.reshape(BLEN, H, DH).astype(jnp.float32)
    value = value.reshape(BLEN, H, DH).astype(jnp.float32)
    inter = jnp.einsum('bhd,hdf->bhf', query, state, precision=lax.Precision.HIGHEST)
    scores = jnp.einsum('bhd,chd->hbc', query, key)
    rows = jnp.arange(BLEN)
    causal = rows[None, :] <= rows[:, None]
    weights = jnp.where(causal[None], scores, 0.0).astype(jnp.bfloat16)
    numerator = inter + jnp.einsum('hbc,chf->bhf', weights.astype(jnp.float32), value)
    meansq = lax.optimization_barrier(jnp.mean(numerator * numerator, axis=-1, keepdims=True))
    normed = (numerator * lax.rsqrt(meansq + 1e-06)).astype(jnp.bfloat16).reshape(BLEN, HD)
    result = jnp.dot(normed, w_out, preferred_element_type=jnp.float32)
    live = rows < live_len
    return jnp.where(live[:, None], result, 0.0).astype(jnp.bfloat16)

def reference(trunk_tokens, branch_tokens, fork_offset, fork_tree, branch_len, w_query, w_key, w_value, w_out):
    all_keys, all_values, prefix = lax.map(lambda tokens: tree_states(tokens, w_key, w_value), trunk_tokens)
    positions = jnp.arange(TRUNK_TOK)

    def one_branch(index):
        owner = index // (N_TRUNK * SLOTS)
        shard = index // SLOTS % N_TRUNK
        within = index % SLOTS
        source = within // CAP
        column = owner * CAP + within % CAP
        offset = fork_offset[source, shard, column]
        tree = source * TREES_DEV + fork_tree[source, shard, column]
        start = (shard * TRUNK_TOK).astype(jnp.int32)
        tree_keys = lax.dynamic_index_in_dim(all_keys, tree, 0, keepdims=False)
        tree_values = lax.dynamic_index_in_dim(all_values, tree, 0, keepdims=False)
        rows_key = lax.dynamic_slice_in_dim(tree_keys, start, TRUNK_TOK, 0).astype(jnp.float32)
        rows_value = lax.dynamic_slice_in_dim(tree_values, start, TRUNK_TOK, 0).astype(jnp.float32)
        keep = (positions < offset).astype(jnp.float32)
        rows_key = (rows_key * keep[:, None]).reshape(TRUNK_TOK, H, DH)
        partial_value = jnp.einsum('thd,thf->hdf', rows_key, rows_value.reshape(TRUNK_TOK, H, DH))
        carried = prefix[tree, shard]
        state = carried + partial_value
        return branch_output(branch_tokens[index], state, branch_len[index], w_query, w_key, w_value, w_out)
    return lax.map(one_branch, jnp.arange(BRANCHES, dtype=jnp.int32))
```

```python
import jax
import jax.numpy as jnp
from jax import lax
from jax.experimental import pallas as pl
from jax.experimental.pallas import tpu as pltpu
from jax.sharding import Mesh
from jax.sharding import PartitionSpec as P

AXES = ("leaf", "ty", "tx", "tc")
TRUNK = AXES[1:]
MESH = pl.DeviceIdType.MESH
BF = jnp.bfloat16
F32 = jnp.float32
H = 8
DH = 128
LEAF = 8
ROW = 4
AHEAD = 3


def dot(left, right):
    return jnp.dot(left, right, preferred_element_type=F32)


def kernel(
    trunk_hbm, branch_hbm, offset, which, wq_hbm, wk_hbm, wv_hbm, wo_hbm,
    normed_hbm, ofull_hbm,
    trunk, branch, kw, vw, qw, ow, key_t, val, tot, crecv, xsend, xrecv, ysend, yrecv,
    own, psend, precv, sbuf, sv, kb, qwb, normed,
    load_sem, kw_load, qo_load, w1s, w1r, w2s, w2r, w3s, w3r, u1s, u1r, u2s, u2r, u3s, u3r,
    cs, cr, xs, xr, ys, yr, ps, pr, zs, zr, out_sem,
):
    leaf = lax.axis_index("leaf")
    ty = lax.axis_index("ty")
    tx = lax.axis_index("tx")
    tc = lax.axis_index("tc")
    here = {"leaf": (leaf, LEAF), "ty": (ty, ROW), "tx": (tx, ROW), "tc": (tc, 2)}

    def peer(axis, k):
        index, size = here[axis]
        return {axis: lax.rem(index + k, size)}

    def remote(src, dst, send, recv, axis, k):
        return pltpu.make_async_remote_copy(
            src_ref=src, dst_ref=dst, send_sem=send, recv_sem=recv,
            device_id=peer(axis, k), device_id_type=MESH,
        )

    def lanes(h, width):
        return pl.ds(pl.multiple_of(h * width, width), width)

    load_trunk = pltpu.make_async_copy(trunk_hbm, trunk, load_sem.at[0])
    load_branch = pltpu.make_async_copy(branch_hbm, branch, load_sem.at[1])

    def load_kv(h):
        return (
            pltpu.make_async_copy(wk_hbm.at[:, lanes(h, DH)], kw.at[h, ty, tx, tc], kw_load.at[h, 0]),
            pltpu.make_async_copy(wv_hbm.at[:, lanes(h, DH)], vw.at[h, ty, tx, tc], kw_load.at[h, 1]),
        )

    def load_qo(p):
        return (
            pltpu.make_async_copy(wq_hbm.at[:, lanes(p, 256)], qw.at[p, ty, tx, tc], qo_load.at[p, 0]),
            pltpu.make_async_copy(wo_hbm.at[:, lanes(p, 256)], ow.at[p, ty, tx, tc], qo_load.at[p, 1]),
        )

    def ways(first, second, s1, r1, s2, r2, s3, r3):
        def one(g):
            out = []
            for k in range(1, ROW):
                a, b = first.at[g, ty, tx, tc], second.at[g, ty, tx, tc]
                out.append(remote(a, a, s1.at[g, k - 1], r1.at[g, k - 1], "tx", k))
                out.append(remote(b, b, s1.at[g, k + 2], r1.at[g, k + 2], "ty", k))
            return out

        def two(g):
            out = []
            for k in range(1, ROW):
                a, b = first.at[g, ty, :, tc], second.at[g, :, tx, tc]
                out.append(remote(a, a, s2.at[g, k - 1], r2.at[g, k - 1], "ty", k))
                out.append(remote(b, b, s2.at[g, k + 2], r2.at[g, k + 2], "tx", k))
            return out

        def three(g):
            a, b = first.at[g, :, :, tc], second.at[g, :, :, tc]
            return [
                remote(a, a, s3.at[g, 0], r3.at[g, 0], "tc", 1),
                remote(b, b, s3.at[g, 1], r3.at[g, 1], "tc", 1),
            ]

        return one, two, three

    kv1, kv2, kv3 = ways(kw, vw, w1s, w1r, w2s, w2r, w3s, w3r)
    qo1, qo2, qo3 = ways(qw, ow, u1s, u1r, u2s, u2r, u3s, u3r)

    def start(copies):
        for c in copies:
            c.start()

    def arrive(copies):
        for c in copies:
            c.wait_recv()

    def sent(copies):
        for c in copies:
            c.wait_send()

    def copy_tot(h):
        return [remote(tot.at[h, 1 - tc], crecv.at[h], cs.at[h], cr.at[h], "tc", 1)]

    def copy_x(h):
        return [
            remote(xsend.at[h], xrecv.at[h, k - 1], xs.at[h, k - 1], xr.at[h, k - 1], "tx", k)
            for k in range(1, ROW)
        ]

    def copy_y(h):
        return [
            remote(ysend.at[h], yrecv.at[h, k - 1], ys.at[h, k - 1], yr.at[h, k - 1], "ty", k)
            for k in range(1, ROW)
        ]

    def copy_p(h):
        return [remote(psend.at[h], precv.at[h], ps.at[h], pr.at[h], "tc", 1)]

    def copy_z(h, k):
        return remote(
            sbuf.at[h, k], sv.at[h, leaf, pl.ds(0, DH)], zs.at[h, k - 1], zr.at[h, k - 1], "leaf", k
        )

    @pl.loop(0, H)
    def _(h):
        start(load_kv(h))

    load_trunk.start()

    @pl.loop(0, 4)
    def _(p):
        start(load_qo(p))

    load_branch.start()

    barrier = pltpu.get_barrier_semaphore()
    partners = (
        [("leaf", k) for k in range(1, LEAF)]
        + [("ty", k) for k in range(1, ROW)]
        + [("tx", k) for k in range(1, ROW)]
        + [("tc", 1)]
    )
    for axis, k in partners:
        pl.semaphore_signal(barrier, inc=1, device_id=peer(axis, k), device_id_type=MESH)
    pl.semaphore_wait(barrier, len(partners))

    @pl.loop(0, H)
    def _(h):
        for c in load_kv(h):
            c.wait()
        start(kv1(h))

    @pl.loop(0, AHEAD)
    def _(h):
        arrive(kv1(h))
        start(kv2(h))

    arrive(kv2(0))
    start(kv3(0))
    load_trunk.wait()

    @pl.loop(0, 4)
    def _(p):
        for c in load_qo(p):
            c.wait()
        start(qo1(p))

    load_branch.wait()

    def weights(h):
        return jnp.concatenate([kw[h].reshape(1024, DH), vw[h].reshape(1024, DH)], axis=1)

    def flag(cond):
        return jnp.where(cond, 1.0, 0.0).astype(F32)

    def stage1(h):
        arrive(kv3(h))
        w = weights(h)
        for r in range(2):
            both = dot(trunk[r], w)
            value = both[:, DH:].astype(BF)
            turned = both[:, :DH].T.astype(BF)
            key_t[h, r] = turned
            val[h, r] = value
            tot[h, r] = dot(turned, value)
        start(copy_tot(h))

    def stage2(h):
        arrive(copy_tot(h))
        xsend[h] = (tot[h, tc] + crecv[h]).astype(BF)
        start(copy_x(h))

    def stage3(h):
        arrive(copy_x(h))
        row = tot[h, tc] + crecv[h]
        for k in range(ROW - 1):
            row = row + xrecv[h, k].astype(F32)
        ysend[h] = row.astype(BF)
        start(copy_y(h))

    def stage4(h):
        arrive(copy_y(h))
        before = jnp.zeros((DH, DH), F32)
        for k in range(1, ROW):
            before = before + flag(ty >= k) * yrecv[h, k - 1].astype(F32)
            before = before + flag(tx >= k) * xrecv[h, k - 1].astype(F32)
        own[h] = before + flag(tc == 1) * crecv[h]
        psend[h] = before + flag(tc == 0) * tot[h, tc]
        start(copy_p(h))

    def stage5(h):
        arrive(copy_p(h))
        position = lax.broadcasted_iota(jnp.int32, (DH, 256), 1)
        for k in (4, 3, 5, 2, 6, 1, 7, 0):
            lane = lax.rem(leaf + k, LEAF)
            tree = which[lane]
            kept = jnp.where(position < offset[lane], key_t[h, tree].astype(F32), 0.0).astype(BF)
            base = jnp.where(tree == tc, own[h], precv[h])
            state = (base + dot(kept, val[h, tree])).astype(BF)
            if k == 0:
                sv[h, leaf, pl.ds(0, DH), :] = state
            else:
                sbuf[h, k] = state
                copy_z(h, k).start()

    def branch_kv(h):
        @pl.loop(0, 4)
        def _(i):
            both = dot(branch[i], weights(h)).astype(BF)
            for j in range(2):
                part = both[j * DH : (j + 1) * DH]
                kb[h, 2 * i + j] = part[:, :DH]
                sv[h, 2 * i + j, pl.ds(DH, DH), :] = part[:, DH:]

    @pl.loop(0, H + 4)
    def _(j):
        @pl.when(j >= 4)
        def _():
            stage5(j - 4)

        @pl.when((j >= 3) & (j < H + 3))
        def _():
            stage4(j - 3)

        @pl.when((j >= 2) & (j < H + 2))
        def _():
            stage3(j - 2)

        @pl.when((j >= 1) & (j < H + 1))
        def _():
            stage2(j - 1)

        @pl.when(j < H)
        def _():
            stage1(j)

        @pl.when(j + AHEAD < H)
        def _():
            arrive(kv1(j + AHEAD))
            start(kv2(j + AHEAD))

        @pl.when(j + 1 < H)
        def _():
            arrive(kv2(j + 1))
            start(kv3(j + 1))

        @pl.when((j >= 4) & (j < 8))
        def _():
            arrive(qo1(j - 4))
            start(qo2(j - 4))

        @pl.when((j >= 6) & (j < 10))
        def _():
            arrive(qo2(j - 6))
            start(qo3(j - 6))

        @pl.when(j < H)
        def _():
            branch_kv(j)

    rows = lax.broadcasted_iota(jnp.int32, (DH, DH), 0)
    columns = lax.broadcasted_iota(jnp.int32, (DH, DH), 1)

    @pl.loop(0, 4)
    def _(p):
        arrive(qo3(p))
        out = pltpu.make_async_copy(ow.at[p], ofull_hbm.at[:, :, :, :, lanes(p, 256)], out_sem.at[p])
        out.start()

        @pl.loop(0, 4)
        def _(i):
            both = dot(branch[i], qw[p].reshape(1024, 256)).astype(BF)
            for j in range(2):
                for u in range(2):
                    qwb[2 * p + u, 2 * i + j, :, pl.ds(0, DH)] = both[
                        j * DH : (j + 1) * DH, u * DH : (u + 1) * DH
                    ]
            for j in range(2):
                for u in range(2):
                    query = both[j * DH : (j + 1) * DH, u * DH : (u + 1) * DH]
                    scores = lax.dot_general(
                        query, kb[2 * p + u, 2 * i + j], (((1,), (1,)), ((), ())), preferred_element_type=F32
                    )
                    qwb[2 * p + u, 2 * i + j, :, pl.ds(DH, DH)] = jnp.where(
                        columns <= rows, scores, 0.0
                    ).astype(BF)

    @pl.loop(0, H)
    def _(h):
        for k in range(1, LEAF):
            copy_z(h, k).wait_recv()

        @pl.loop(0, LEAF)
        def _(s):
            numerator = dot(qwb[h, s], sv[h, s])
            meansq = jnp.mean(numerator * numerator, axis=-1, keepdims=True)
            normed[s, :, lanes(h, DH)] = (numerator * lax.rsqrt(meansq + 1e-06)).astype(BF)

        out = pltpu.make_async_copy(
            normed.at[:, :, lanes(h, DH)], normed_hbm.at[:, :, lanes(h, DH)], out_sem.at[4 + h]
        )
        out.start()

    @pl.loop(0, H)
    def _(h):
        sent(kv1(h) + kv2(h) + kv3(h) + copy_tot(h) + copy_x(h) + copy_y(h) + copy_p(h))
        sent([copy_z(h, k) for k in range(1, LEAF)])
        pltpu.make_async_copy(
            normed.at[:, :, lanes(h, DH)], normed_hbm.at[:, :, lanes(h, DH)], out_sem.at[4 + h]
        ).wait()

    @pl.loop(0, 4)
    def _(p):
        sent(qo1(p) + qo2(p) + qo3(p))
        pltpu.make_async_copy(
            ow.at[p], ofull_hbm.at[:, :, :, :, lanes(p, 256)], out_sem.at[p]
        ).wait()


def shards(
    trunk_tokens, branch_tokens, fork_offset, fork_tree, branch_len, w_query, w_key, w_value, w_out
):
    slots, blen, width = branch_tokens.shape
    dma = pltpu.SemaphoreType.DMA
    anywhere = pl.BlockSpec(memory_space=pl.ANY)
    small = pl.BlockSpec(memory_space=pltpu.SMEM)
    square = (DH, DH)
    vm = pltpu.VMEM
    normed, ofull = pl.pallas_call(
        kernel,
        out_shape=(
            jax.ShapeDtypeStruct((slots, blen, H * DH), BF),
            jax.ShapeDtypeStruct((ROW, ROW, 2, 32, width), BF),
        ),
        in_specs=[anywhere, anywhere, small, small] + [anywhere] * 4,
        out_specs=(anywhere, anywhere),
        scratch_shapes=[
            vm((2, 256, 1024), BF),
            vm((4, 256, 1024), BF),
            vm((H, ROW, ROW, 2, 32, DH), BF),
            vm((H, ROW, ROW, 2, 32, DH), BF),
            vm((4, ROW, ROW, 2, 32, 256), BF),
            vm((4, ROW, ROW, 2, 32, 256), BF),
            vm((H, 2, DH, 256), BF),
            vm((H, 2, 256, DH), BF),
            vm((H, 2) + square, F32),
            vm((H,) + square, F32),
            vm((H,) + square, BF),
            vm((H, ROW - 1) + square, BF),
            vm((H,) + square, BF),
            vm((H, ROW - 1) + square, BF),
            vm((H,) + square, F32),
            vm((H,) + square, F32),
            vm((H,) + square, F32),
            vm((H, LEAF) + square, BF),
            vm((H, LEAF, 256, DH), BF),
            vm((H, LEAF) + square, BF),
            vm((H, LEAF, DH, 256), BF),
            vm((LEAF, DH, H * DH), BF),
            dma((2,)), dma((H, 2)), dma((4, 2)),
            dma((H, 6)), dma((H, 6)), dma((H, 6)), dma((H, 6)), dma((H, 2)), dma((H, 2)),
            dma((4, 6)), dma((4, 6)), dma((4, 6)), dma((4, 6)), dma((4, 2)), dma((4, 2)),
            dma((H,)), dma((H,)), dma((H, 3)), dma((H, 3)), dma((H, 3)), dma((H, 3)), dma((H,)), dma((H,)),
            dma((H, 7)), dma((H, 7)), dma((12,)),
        ],
        compiler_params=pltpu.CompilerParams(
            collective_id=0, has_side_effects=True, vmem_limit_bytes=56 << 20
        ),
    )(
        trunk_tokens, branch_tokens.reshape(4, 256, width), fork_offset.reshape(-1), fork_tree.reshape(-1),
        w_query, w_key, w_value, w_out,
    )
    projected = jnp.dot(
        normed.reshape(slots * blen, H * DH), ofull.reshape(H * DH, width), preferred_element_type=F32
    )
    rows = jnp.arange(blen, dtype=jnp.int32)
    live = rows[None, :] < branch_len[:, None]
    projected = projected.reshape(slots, blen, width)
    return jnp.where(live[:, :, None], projected, 0.0).astype(BF)


def solution(mesh):
    split = Mesh(mesh.devices.reshape(LEAF, ROW, ROW, 2), AXES)
    return jax.shard_map(
        shards,
        mesh=split,
        in_specs=(
            P("leaf", TRUNK, None),
            P(AXES, None, None),
            P("leaf", TRUNK, None),
            P("leaf", TRUNK, None),
            P(AXES),
            P(TRUNK, None),
            P(TRUNK, None),
            P(TRUNK, None),
            P(TRUNK, None),
        ),
        out_specs=P(AXES, None, None),
        check_vma=False,
    )
```

```python
import jax
import jax.numpy as jnp
from jax import lax
from jax.experimental import pallas as pl
from jax.experimental.pallas import tpu as pltpu
from jax.sharding import Mesh
from jax.sharding import PartitionSpec as P

AXES = ("leaf", "ty", "tx", "tc")
TRUNK = AXES[1:]
MESH = pl.DeviceIdType.MESH
BF = jnp.bfloat16
F32 = jnp.float32
H = 8
DH = 128
LEAF = 8
ROW = 4


def dot(left, right):
    return jnp.dot(left, right, preferred_element_type=F32)


def kernel(
    trunk_hbm, branch_hbm, offset, which, length, wq_hbm, wk_hbm, wv_hbm, wo_hbm,
    result,
    trunk, branch, kw, vw, qw, ow, key_t, val, tot, crecv, xsend, xrecv, ysend, yrecv,
    carried, psend, sbuf, sv, kb, qwb, normed, acc,
    load_sem, w1r, w2r, w3r, u1r, u2r, u3r, cr, xr, yr, pr, zr, send, near,
):
    leaf = lax.axis_index("leaf")
    ty = lax.axis_index("ty")
    tx = lax.axis_index("tx")
    tc = lax.axis_index("tc")
    here = {"leaf": (leaf, LEAF), "ty": (ty, ROW), "tx": (tx, ROW), "tc": (tc, 2)}

    def peer(axis, k):
        index, size = here[axis]
        return {axis: lax.rem(index + k, size)}

    def remote(src, dst, send, recv, axis, k):
        return pltpu.make_async_remote_copy(
            src_ref=src, dst_ref=dst, send_sem=send, recv_sem=recv,
            device_id=peer(axis, k), device_id_type=MESH,
        )

    def lanes(h, width):
        return pl.ds(pl.multiple_of(h * width, width), width)

    def landed(view, sem):
        pltpu.make_async_copy(view, view, sem).wait()

    load_trunk = pltpu.make_async_copy(trunk_hbm, trunk, load_sem.at[0])
    load_branch = pltpu.make_async_copy(branch_hbm, branch, load_sem.at[1])

    def load_kv(h):
        pltpu.make_async_copy(wk_hbm.at[:, lanes(h, DH)], kw.at[h, ty, tx, tc], load_sem.at[2]).start()
        pltpu.make_async_copy(wv_hbm.at[:, lanes(h, DH)], vw.at[h, ty, tx, tc], load_sem.at[2]).start()

    def load_qo(p):
        pltpu.make_async_copy(wq_hbm.at[:, lanes(p, 256)], qw.at[p, ty, tx, tc], load_sem.at[3]).start()
        pltpu.make_async_copy(wo_hbm.at[:, lanes(p, 256)], ow.at[p, ty, tx, tc], load_sem.at[3]).start()

    def ways(first, second, s, r1, r2, r3):
        def one(g):
            for k in (2, 1, 3):
                a, b = first.at[g, ty, tx, tc], second.at[g, ty, tx, tc]
                remote(a, a, send.at[s], r1.at[g], "tx", k).start()
                remote(b, b, send.at[s], r1.at[g], "ty", k).start()

        def two(g):
            landed(first.at[0, 0, pl.ds(0, 3)], r1.at[g])
            for k in (2, 1, 3):
                a, b = first.at[g, ty, :, tc], second.at[g, :, tx, tc]
                remote(a, a, send.at[s + 1], r2.at[g], "ty", k).start()
                remote(b, b, send.at[s + 1], r2.at[g], "tx", k).start()

        def three(g):
            landed(first.at[0, pl.ds(0, 3)], r2.at[g])
            a, b = first.at[g, :, :, tc], second.at[g, :, :, tc]
            remote(a, a, send.at[s + 2], r3.at[g], "tc", 1).start()
            remote(b, b, send.at[s + 2], r3.at[g], "tc", 1).start()

        def ready(g):
            landed(first.at[0], r3.at[g])

        return one, two, three, ready

    kv_first, kv_second, kv_third, kv_ready = ways(kw, vw, 0, w1r, w2r, w3r)
    qo_first, qo_second, qo_third, qo_ready = ways(qw, ow, 3, u1r, u2r, u3r)

    def send_tot(h):
        remote(tot.at[h, 1 - tc], crecv.at[h], send.at[6], cr.at[h], "tc", 1).start()

    def send_x(h):
        for k in (2, 1, 3):
            remote(xsend.at[h], xrecv.at[h, k - 1], send.at[7], xr.at[h], "tx", k).start()

    def send_y(h):
        for k in (2, 1, 3):
            remote(ysend.at[h], yrecv.at[h, k - 1], send.at[8], yr.at[h], "ty", k).start()

    def send_p(h):
        remote(psend.at[h], carried.at[h, 1], send.at[9], pr.at[h], "tc", 1).start()

    def send_z(h, k):
        remote(sbuf.at[h, k], sv.at[h, leaf, pl.ds(0, DH)], send.at[10], zr.at[h], "leaf", k).start()

    barrier = pltpu.get_barrier_semaphore()
    partners = [("tc", 1), ("leaf", 1), ("leaf", LEAF - 1)]
    partners += [(axis, k) for axis in ("tx", "ty") for k in range(1, ROW)]
    for axis, k in partners:
        pl.semaphore_signal(barrier, inc=1, device_id=peer(axis, k), device_id_type=MESH)

    def vouch(i):
        for k in (1, LEAF - 1):
            pl.semaphore_signal(near.at[i], inc=1, device_id=peer("leaf", k), device_id_type=MESH)

    @pl.loop(0, H)
    def _(h):
        load_kv(h)

    load_trunk.start()
    load_branch.start()

    @pl.loop(0, 4)
    def _(p):
        load_qo(p)

    pl.semaphore_wait(barrier, len(partners))
    landed(kw.at[0, pl.ds(0, 2)], load_sem.at[2])
    kv_first(0)
    vouch(0)

    @pl.loop(1, 4)
    def _(h):
        kv_first(h)

    kv_second(0)
    kv_third(0)

    @pl.loop(1, 4)
    def _(h):
        kv_second(h)

    @pl.loop(4, H)
    def _(h):
        kv_first(h)

    load_trunk.wait()
    load_branch.wait()
    landed(qw.at[0, 0], load_sem.at[3])
    pl.semaphore_wait(near.at[0], 2)
    vouch(1)

    def weights(h):
        return jnp.concatenate([kw[h].reshape(1024, DH), vw[h].reshape(1024, DH)], axis=1)

    def flag(cond):
        return jnp.where(cond, 1.0, 0.0).astype(F32)

    def stage1(h):
        kv_ready(h)
        both = dot(trunk[...], weights(h))
        for r in range(2):
            part = both[r * 256 : (r + 1) * 256]
            value = part[:, DH:].astype(BF)
            turned = part[:, :DH].T.astype(BF)
            key_t[h, r] = turned
            val[h, r] = value
            tot[h, r] = dot(turned, value)
        send_tot(h)

    def stage2(h):
        landed(crecv.at[h], cr.at[h])
        xsend[h] = (tot[h, tc] + crecv[h]).astype(BF)
        send_x(h)

    def stage3(h):
        landed(xrecv.at[h], xr.at[h])
        row = tot[h, tc] + crecv[h]
        for k in range(ROW - 1):
            row = row + xrecv[h, k].astype(F32)
        ysend[h] = row.astype(BF)
        send_y(h)

    def stage4(h):
        landed(yrecv.at[h], yr.at[h])
        before = jnp.zeros((DH, DH), F32)
        for k in range(1, ROW):
            before = before + flag(ty >= k) * yrecv[h, k - 1].astype(F32)
            before = before + flag(tx >= k) * xrecv[h, k - 1].astype(F32)
        psend[h] = before + flag(tc == 0) * tot[h, tc]
        send_p(h)
        carried[h, 0] = before + flag(tc == 1) * crecv[h]

    shifts = (4, 3, 5, 2, 6, 1, 7, 0)

    def stage5(h):
        landed(psend.at[h], pr.at[h])
        position = lax.broadcasted_iota(jnp.int32, (DH, 256), 1)
        for k in shifts:
            lane = lax.rem(leaf + k, LEAF)
            tree = which[lane]
            kept = jnp.where(position < offset[lane], key_t[h, tree].astype(F32), 0.0).astype(BF)
            base = jnp.where(tree == tc, carried[h, 0], carried[h, 1])
            state = (base + dot(kept, val[h, tree])).astype(BF)
            if k == 0:
                sv[h, leaf, pl.ds(0, DH), :] = state
            else:
                sbuf[h, k] = state
        for k in shifts[:-1]:
            send_z(h, k)

    def branch_kv(h):
        both = dot(branch[...], weights(h)).astype(BF)
        for s in range(LEAF):
            part = both[s * DH : (s + 1) * DH]
            kb[h, s] = part[:, :DH]
            sv[h, s, pl.ds(DH, DH), :] = part[:, DH:]

    rows = lax.broadcasted_iota(jnp.int32, (DH, DH), 0)
    columns = lax.broadcasted_iota(jnp.int32, (DH, DH), 1)

    def branch_q(p):
        qo_ready(p)
        both = dot(branch[...], qw[p].reshape(1024, 256)).astype(BF)
        for s in range(LEAF):
            for u in range(2):
                query = both[s * DH : (s + 1) * DH, u * DH : (u + 1) * DH]
                scores = lax.dot_general(
                    query, kb[2 * p + u, s], (((1,), (1,)), ((), ())), preferred_element_type=F32
                )
                qwb[2 * p + u, s, :, pl.ds(0, DH)] = query
                qwb[2 * p + u, s, :, pl.ds(DH, DH)] = jnp.where(columns <= rows, scores, 0.0).astype(BF)

    @pl.loop(0, H + 4)
    def _(j):
        @pl.when(j < H)
        def _():
            stage1(j)
            branch_kv(j)

        @pl.when(j + 1 < H)
        def _():
            kv_third(j + 1)

        @pl.when(j == 0)
        def _():
            pl.semaphore_wait(near.at[1], 2)
            vouch(2)

        @pl.when((j >= 2) & (j < H + 2))
        def _():
            stage4(j - 2)

        @pl.when((j >= 1) & (j < H + 1))
        def _():
            stage3(j - 1)

        @pl.when(j < H)
        def _():
            stage2(j)

        @pl.when(j == 1)
        def _():
            pl.semaphore_wait(near.at[2], 2)

        @pl.when(j >= 8)
        def _():
            branch_q(j - 8)

        @pl.when((j >= 2) & (j < H + 2))
        def _():
            stage5(j - 2)

        @pl.when((j >= 2) & (j < 4))
        def _():
            kv_second(2 * j)
            kv_second(2 * j + 1)

        @pl.when((j >= 3) & (j < 7))
        def _():
            qo_first(j - 3)

        @pl.when((j >= 5) & (j < 9))
        def _():
            qo_second(j - 5)

        @pl.when((j >= 7) & (j < 11))
        def _():
            qo_third(j - 7)

    def finish(p):
        for u in range(2):
            h = 2 * p + u
            landed(sbuf.at[h, pl.ds(0, LEAF - 1)], zr.at[h])
            for s in range(LEAF):
                numerator = dot(qwb[h, s], sv[h, s])
                meansq = jnp.mean(numerator * numerator, axis=-1, keepdims=True)
                normed[s * DH : (s + 1) * DH, u * DH : (u + 1) * DH] = (
                    numerator * lax.rsqrt(meansq + 1e-06)
                ).astype(BF)

    def product(p, c):
        return dot(normed[...], ow[c, p].reshape(256, 256))

    landed(kw.at[pl.ds(0, 3), pl.ds(0, 2)], send.at[0])
    landed(kw.at[pl.ds(0, 6)], send.at[1])
    landed(kw, send.at[2])
    landed(qw.at[0, pl.ds(0, 3)], send.at[3])
    landed(qw.at[pl.ds(0, 3)], send.at[4])
    landed(qw, send.at[5])
    landed(crecv, send.at[6])
    landed(xrecv, send.at[7])
    landed(yrecv, send.at[8])
    landed(psend, send.at[9])

    finish(0)
    for c in range(4):
        acc[c] = product(0, c)

    @pl.loop(1, 3)
    def _(p):
        finish(p)
        for c in range(4):
            acc[c] += product(p, c)

    finish(3)
    place = lax.broadcasted_iota(jnp.int32, (DH, 256), 0)
    for c in range(4):
        total = acc[c] + product(3, c)
        for s in range(LEAF):
            result[s, :, c * 256 : (c + 1) * 256] = jnp.where(
                place < length[s], total[s * DH : (s + 1) * DH], 0.0
            ).astype(BF)

    landed(sbuf.at[pl.ds(0, LEAF - 1)], send.at[10])


def shards(
    trunk_tokens, branch_tokens, fork_offset, fork_tree, branch_len, w_query, w_key, w_value, w_out
):
    slots, blen, width = branch_tokens.shape
    dma = pltpu.SemaphoreType.DMA
    anywhere = pl.BlockSpec(memory_space=pltpu.HBM)
    small = pl.BlockSpec(memory_space=pltpu.SMEM)
    square = (DH, DH)
    vm = pltpu.VMEM
    return pl.pallas_call(
        kernel,
        out_shape=pltpu.VMEM((slots, blen, width), BF),
        in_specs=[anywhere, anywhere, small, small, small] + [anywhere] * 4,
        out_specs=pl.BlockSpec(memory_space=pltpu.VMEM),
        scratch_shapes=[
            vm((512, 1024), BF),
            vm((1024, 1024), BF),
            vm((H, ROW, ROW, 2, 32, DH), BF),
            vm((H, ROW, ROW, 2, 32, DH), BF),
            vm((4, ROW, ROW, 2, 32, 256), BF),
            vm((4, ROW, ROW, 2, 32, 256), BF),
            vm((H, 2, DH, 256), BF),
            vm((H, 2, 256, DH), BF),
            vm((H, 2) + square, F32),
            vm((H,) + square, F32),
            vm((H,) + square, BF),
            vm((H, ROW - 1) + square, BF),
            vm((H,) + square, BF),
            vm((H, ROW - 1) + square, BF),
            vm((H, 2) + square, F32),
            vm((H,) + square, F32),
            vm((H, LEAF) + square, BF),
            vm((H, LEAF, 256, DH), BF),
            vm((H, LEAF) + square, BF),
            vm((H, LEAF, DH, 256), BF),
            vm((1024, 256), BF),
            vm((4, 1024, 256), F32),
            dma((4,)),
            dma((H,)), dma((H,)), dma((H,)), dma((4,)), dma((4,)), dma((4,)),
            dma((H,)), dma((H,)), dma((H,)), dma((H,)), dma((H,)),
            dma((11,)), pltpu.SemaphoreType.REGULAR((3,)),
        ],
        compiler_params=pltpu.CompilerParams(
            collective_id=0, has_side_effects=True, vmem_limit_bytes=60 << 20
        ),
    )(
        trunk_tokens.reshape(-1, width), branch_tokens.reshape(-1, width),
        fork_offset.reshape(-1), fork_tree.reshape(-1), branch_len,
        w_query, w_key, w_value, w_out,
    )


def solution(mesh):
    split = Mesh(mesh.devices.reshape(LEAF, ROW, ROW, 2), AXES)
    return jax.shard_map(
        shards,
        mesh=split,
        in_specs=(
            P("leaf", TRUNK, None),
            P(AXES, None, None),
            P("leaf", TRUNK, None),
            P("leaf", TRUNK, None),
            P(AXES),
            P(TRUNK, None),
            P(TRUNK, None),
            P(TRUNK, None),
            P(TRUNK, None),
        ),
        out_specs=P(AXES, None, None),
        check_vma=False,
    )
```

```python
import jax
import jax.numpy as jnp
from jax import lax
from jax.experimental import pallas as pl
from jax.experimental.pallas import tpu as pltpu
from jax.sharding import Mesh
from jax.sharding import PartitionSpec as P

AXES = ("leaf", "ty", "tx", "tc")
TRUNK = AXES[1:]
MESH = pl.DeviceIdType.MESH
BF = jnp.bfloat16
F32 = jnp.float32
H = 8
DH = 128
LEAF = 8
ROW = 4


def dot(left, right):
    return jnp.dot(left, right, preferred_element_type=F32)


def kernel(
    trunk_hbm, branch_hbm, offset, which, length, wq_hbm, wk_hbm, wv_hbm, wo_hbm,
    result,
    trunk, branch, kw, vw, qw, ow, key_t, val, tot, crecv, xsend, xrecv, ysend, yrecv,
    carried, psend, sbuf, sv, kb, qwb, normed, acc,
    load_sem, w1r, w2r, w3r, u1r, u2r, u3r, cr, xr, yr, pr, zr, send, near,
):
    leaf = lax.axis_index("leaf")
    ty = lax.axis_index("ty")
    tx = lax.axis_index("tx")
    tc = lax.axis_index("tc")
    here = {"leaf": (leaf, LEAF), "ty": (ty, ROW), "tx": (tx, ROW), "tc": (tc, 2)}

    def peer(axis, k):
        index, size = here[axis]
        return {axis: lax.rem(index + k, size)}

    def remote(src, dst, send, recv, axis, k):
        return pltpu.make_async_remote_copy(
            src_ref=src, dst_ref=dst, send_sem=send, recv_sem=recv,
            device_id=peer(axis, k), device_id_type=MESH,
        )

    def lanes(h, width):
        return pl.ds(pl.multiple_of(h * width, width), width)

    def landed(view, sem):
        pltpu.make_async_copy(view, view, sem).wait()

    load_trunk = pltpu.make_async_copy(trunk_hbm, trunk, load_sem.at[0])
    load_branch = pltpu.make_async_copy(branch_hbm, branch, load_sem.at[1])

    def load_kv(h):
        pltpu.make_async_copy(wk_hbm.at[:, lanes(h, DH)], kw.at[h, ty, tx, tc], load_sem.at[2]).start()
        pltpu.make_async_copy(wv_hbm.at[:, lanes(h, DH)], vw.at[h, ty, tx, tc], load_sem.at[2]).start()

    def load_qo(p):
        pltpu.make_async_copy(wq_hbm.at[:, lanes(p, 256)], qw.at[p, ty, tx, tc], load_sem.at[3]).start()
        pltpu.make_async_copy(wo_hbm.at[:, lanes(p, 256)], ow.at[p, ty, tx, tc], load_sem.at[3]).start()

    def ways(first, second, s, r1, r2, r3):
        def one(g):
            for k in (2, 1, 3):
                a, b = first.at[g, ty, tx, tc], second.at[g, ty, tx, tc]
                remote(a, a, send.at[s], r1.at[g], "tx", k).start()
                remote(b, b, send.at[s], r1.at[g], "ty", k).start()

        def two(g):
            landed(first.at[0, 0, pl.ds(0, 3)], r1.at[g])
            for k in (2, 1, 3):
                a, b = first.at[g, ty, :, tc], second.at[g, :, tx, tc]
                remote(a, a, send.at[s + 1], r2.at[g], "ty", k).start()
                remote(b, b, send.at[s + 1], r2.at[g], "tx", k).start()

        def three(g):
            landed(first.at[0, pl.ds(0, 3)], r2.at[g])
            a, b = first.at[g, :, :, tc], second.at[g, :, :, tc]
            remote(a, a, send.at[s + 2], r3.at[g], "tc", 1).start()
            remote(b, b, send.at[s + 2], r3.at[g], "tc", 1).start()

        def ready(g):
            landed(first.at[0], r3.at[g])

        return one, two, three, ready

    kv_first, kv_second, kv_third, kv_ready = ways(kw, vw, 0, w1r, w2r, w3r)
    qo_first, qo_second, qo_third, qo_ready = ways(qw, ow, 3, u1r, u2r, u3r)

    def send_tot(h):
        remote(tot.at[h, 1 - tc], crecv.at[h], send.at[6], cr.at[h], "tc", 1).start()

    def send_x(h):
        for k in (2, 1, 3):
            remote(xsend.at[h], xrecv.at[h, k - 1], send.at[7], xr.at[h], "tx", k).start()

    def send_y(h):
        for k in (2, 1, 3):
            remote(ysend.at[h], yrecv.at[h, k - 1], send.at[8], yr.at[h], "ty", k).start()

    def send_p(h):
        remote(psend.at[h], carried.at[h, 1], send.at[9], pr.at[h], "tc", 1).start()

    def send_z(h, k):
        remote(sbuf.at[h, k], sv.at[h, leaf, pl.ds(0, DH)], send.at[10], zr.at[h], "leaf", k).start()

    barrier = pltpu.get_barrier_semaphore()
    partners = [("tc", 1), ("leaf", 1), ("leaf", LEAF - 1)]
    partners += [(axis, k) for axis in ("tx", "ty") for k in range(1, ROW)]
    for axis, k in partners:
        pl.semaphore_signal(barrier, inc=1, device_id=peer(axis, k), device_id_type=MESH)

    def vouch(i):
        for k in (1, LEAF - 1):
            pl.semaphore_signal(near.at[i], inc=1, device_id=peer("leaf", k), device_id_type=MESH)

    @pl.loop(0, H)
    def _(h):
        load_kv(h)

    load_trunk.start()
    load_branch.start()

    @pl.loop(0, 4)
    def _(p):
        load_qo(p)

    pl.semaphore_wait(barrier, len(partners))
    landed(kw.at[0, pl.ds(0, 2)], load_sem.at[2])
    kv_first(0)
    vouch(0)

    @pl.loop(1, 4)
    def _(h):
        kv_first(h)

    kv_second(0)
    kv_third(0)

    @pl.loop(1, 4)
    def _(h):
        kv_second(h)

    @pl.loop(4, H)
    def _(h):
        kv_first(h)

    load_trunk.wait()
    load_branch.wait()
    landed(qw.at[0, 0], load_sem.at[3])

    def weights(h):
        return jnp.concatenate([kw[h].reshape(1024, DH), vw[h].reshape(1024, DH)], axis=1)

    def flag(cond):
        return jnp.where(cond, 1.0, 0.0).astype(F32)

    def stage1(h):
        kv_ready(h)
        both = dot(trunk[...], weights(h))
        for r in range(2):
            part = both[r * 256 : (r + 1) * 256]
            value = part[:, DH:].astype(BF)
            turned = part[:, :DH].T.astype(BF)
            key_t[h, r] = turned
            val[h, r] = value
            tot[h, r] = dot(turned, value)
        send_tot(h)

    def stage2(h):
        landed(crecv.at[h], cr.at[h])
        xsend[h] = (tot[h, tc] + crecv[h]).astype(BF)
        send_x(h)

    def stage3(h):
        landed(xrecv.at[h], xr.at[h])
        row = tot[h, tc] + crecv[h]
        for k in range(ROW - 1):
            row = row + xrecv[h, k].astype(F32)
        ysend[h] = row.astype(BF)
        send_y(h)

    def stage4(h):
        landed(yrecv.at[h], yr.at[h])
        before = jnp.zeros((DH, DH), F32)
        for k in range(1, ROW):
            before = before + flag(ty >= k) * yrecv[h, k - 1].astype(F32)
            before = before + flag(tx >= k) * xrecv[h, k - 1].astype(F32)
        psend[h] = before + flag(tc == 0) * tot[h, tc]
        send_p(h)
        carried[h, 0] = before + flag(tc == 1) * crecv[h]

    shifts = (4, 3, 5, 2, 6, 1, 7, 0)

    def stage5(h):
        landed(psend.at[h], pr.at[h])
        position = lax.broadcasted_iota(jnp.int32, (DH, 256), 1)
        for k in shifts:
            lane = lax.rem(leaf + k, LEAF)
            tree = which[lane]
            kept = jnp.where(position < offset[lane], key_t[h, tree].astype(F32), 0.0).astype(BF)
            base = jnp.where(tree == tc, carried[h, 0], carried[h, 1])
            state = (base + dot(kept, val[h, tree])).astype(BF)
            if k == 0:
                sv[h, leaf, pl.ds(0, DH), :] = state
            else:
                sbuf[h, k] = state
        for k in shifts[:-1]:
            send_z(h, k)

    def branch_kv(h):
        both = dot(branch[...], weights(h)).astype(BF)
        for s in range(LEAF):
            part = both[s * DH : (s + 1) * DH]
            kb[h, s] = part[:, :DH]
            sv[h, s, pl.ds(DH, DH), :] = part[:, DH:]

    rows = lax.broadcasted_iota(jnp.int32, (DH, DH), 0)
    columns = lax.broadcasted_iota(jnp.int32, (DH, DH), 1)

    def branch_q(p):
        qo_ready(p)
        both = dot(branch[...], qw[p].reshape(1024, 256)).astype(BF)
        for s in range(LEAF):
            for u in range(2):
                query = both[s * DH : (s + 1) * DH, u * DH : (u + 1) * DH]
                scores = lax.dot_general(
                    query, kb[2 * p + u, s], (((1,), (1,)), ((), ())), preferred_element_type=F32
                )
                qwb[2 * p + u, s, :, pl.ds(0, DH)] = query
                qwb[2 * p + u, s, :, pl.ds(DH, DH)] = jnp.where(columns <= rows, scores, 0.0).astype(BF)

    @pl.loop(0, H + 4)
    def _(j):
        @pl.when(j < H)
        def _():
            stage1(j)

        @pl.when((j >= 2) & (j < H + 2))
        def _():
            stage4(j - 2)

        @pl.when((j >= 1) & (j < H + 1))
        def _():
            stage3(j - 1)

        @pl.when(j < H)
        def _():
            stage2(j)

        @pl.when(j == 0)
        def _():
            pl.semaphore_wait(near.at[0], 2)
            vouch(1)

        @pl.when(j == 1)
        def _():
            pl.semaphore_wait(near.at[1], 2)
            vouch(2)

        @pl.when(j == 2)
        def _():
            pl.semaphore_wait(near.at[2], 2)

        @pl.when(j >= 8)
        def _():
            branch_q(j - 8)

        @pl.when((j >= 2) & (j < H + 2))
        def _():
            stage5(j - 2)

        @pl.when(j + 1 < H)
        def _():
            kv_third(j + 1)

        @pl.when((j >= 2) & (j < 4))
        def _():
            kv_second(2 * j)
            kv_second(2 * j + 1)

        @pl.when((j >= 3) & (j < 7))
        def _():
            qo_first(j - 3)

        @pl.when((j >= 5) & (j < 9))
        def _():
            qo_second(j - 5)

        @pl.when((j >= 7) & (j < 11))
        def _():
            qo_third(j - 7)

        @pl.when(j < H)
        def _():
            branch_kv(j)

    def finish(p):
        for u in range(2):
            h = 2 * p + u
            landed(sbuf.at[h, pl.ds(0, LEAF - 1)], zr.at[h])
            for s in range(LEAF):
                numerator = dot(qwb[h, s], sv[h, s])
                meansq = jnp.mean(numerator * numerator, axis=-1, keepdims=True)
                normed[s * DH : (s + 1) * DH, u * DH : (u + 1) * DH] = (
                    numerator * lax.rsqrt(meansq + 1e-06)
                ).astype(BF)

    def product(p, c):
        return dot(normed[...], ow[c, p].reshape(256, 256))

    landed(kw.at[pl.ds(0, 3), pl.ds(0, 2)], send.at[0])
    landed(kw.at[pl.ds(0, 6)], send.at[1])
    landed(kw, send.at[2])
    landed(qw.at[0, pl.ds(0, 3)], send.at[3])
    landed(qw.at[pl.ds(0, 3)], send.at[4])
    landed(qw, send.at[5])
    landed(crecv, send.at[6])
    landed(xrecv, send.at[7])
    landed(yrecv, send.at[8])
    landed(psend, send.at[9])

    finish(0)
    for c in range(4):
        acc[c] = product(0, c)

    @pl.loop(1, 3)
    def _(p):
        finish(p)
        for c in range(4):
            acc[c] += product(p, c)

    finish(3)
    place = lax.broadcasted_iota(jnp.int32, (DH, 256), 0)
    for c in range(4):
        total = acc[c] + product(3, c)
        for s in range(LEAF):
            result[s, :, c * 256 : (c + 1) * 256] = jnp.where(
                place < length[s], total[s * DH : (s + 1) * DH], 0.0
            ).astype(BF)

    landed(sbuf.at[pl.ds(0, LEAF - 1)], send.at[10])


def shards(
    trunk_tokens, branch_tokens, fork_offset, fork_tree, branch_len, w_query, w_key, w_value, w_out
):
    slots, blen, width = branch_tokens.shape
    dma = pltpu.SemaphoreType.DMA
    anywhere = pl.BlockSpec(memory_space=pltpu.HBM)
    small = pl.BlockSpec(memory_space=pltpu.SMEM)
    square = (DH, DH)
    vm = pltpu.VMEM
    return pl.pallas_call(
        kernel,
        out_shape=pltpu.VMEM((slots, blen, width), BF),
        in_specs=[anywhere, anywhere, small, small, small] + [anywhere] * 4,
        out_specs=pl.BlockSpec(memory_space=pltpu.VMEM),
        scratch_shapes=[
            vm((512, 1024), BF),
            vm((1024, 1024), BF),
            vm((H, ROW, ROW, 2, 32, DH), BF),
            vm((H, ROW, ROW, 2, 32, DH), BF),
            vm((4, ROW, ROW, 2, 32, 256), BF),
            vm((4, ROW, ROW, 2, 32, 256), BF),
            vm((H, 2, DH, 256), BF),
            vm((H, 2, 256, DH), BF),
            vm((H, 2) + square, F32),
            vm((H,) + square, F32),
            vm((H,) + square, BF),
            vm((H, ROW - 1) + square, BF),
            vm((H,) + square, BF),
            vm((H, ROW - 1) + square, BF),
            vm((H, 2) + square, F32),
            vm((H,) + square, F32),
            vm((H, LEAF) + square, BF),
            vm((H, LEAF, 256, DH), BF),
            vm((H, LEAF) + square, BF),
            vm((H, LEAF, DH, 256), BF),
            vm((1024, 256), BF),
            vm((4, 1024, 256), F32),
            dma((4,)),
            dma((H,)), dma((H,)), dma((H,)), dma((4,)), dma((4,)), dma((4,)),
            dma((H,)), dma((H,)), dma((H,)), dma((H,)), dma((H,)),
            dma((11,)), pltpu.SemaphoreType.REGULAR((3,)),
        ],
        compiler_params=pltpu.CompilerParams(
            collective_id=0, has_side_effects=True, vmem_limit_bytes=60 << 20
        ),
    )(
        trunk_tokens.reshape(-1, width), branch_tokens.reshape(-1, width),
        fork_offset.reshape(-1), fork_tree.reshape(-1), branch_len,
        w_query, w_key, w_value, w_out,
    )


def solution(mesh):
    split = Mesh(mesh.devices.reshape(LEAF, ROW, ROW, 2), AXES)
    return jax.shard_map(
        shards,
        mesh=split,
        in_specs=(
            P("leaf", TRUNK, None),
            P(AXES, None, None),
            P("leaf", TRUNK, None),
            P("leaf", TRUNK, None),
            P(AXES),
            P(TRUNK, None),
            P(TRUNK, None),
            P(TRUNK, None),
            P(TRUNK, None),
        ),
        out_specs=P(AXES, None, None),
        check_vma=False,
    )
```

```python
import jax
import jax.numpy as jnp
from jax import lax
from jax.experimental import pallas as pl
from jax.experimental.pallas import tpu as pltpu
from jax.sharding import Mesh
from jax.sharding import PartitionSpec as P

AXES = ("leaf", "ty", "tx", "tc")
TRUNK = AXES[1:]
MESH = pl.DeviceIdType.MESH
BF = jnp.bfloat16
F32 = jnp.float32
H = 8
DH = 128
LEAF = 8
ROW = 4


def dot(left, right):
    return jnp.dot(left, right, preferred_element_type=F32)


def kernel(
    trunk_hbm, branch_hbm, offset, which, length, wq_hbm, wk_hbm, wv_hbm, wo_hbm,
    result,
    trunk, branch, kw, vw, qw, ow, key_t, val, tot, crecv, xsend, xrecv, ysend, yrecv,
    carried, psend, sbuf, sv, kb, qwb, normed, acc,
    load_sem, w1r, w2r, w3r, u1r, u2r, u3r, cr, xr, yr, pr, zr, send, near,
):
    leaf = lax.axis_index("leaf")
    ty = lax.axis_index("ty")
    tx = lax.axis_index("tx")
    tc = lax.axis_index("tc")
    here = {"leaf": (leaf, LEAF), "ty": (ty, ROW), "tx": (tx, ROW), "tc": (tc, 2)}

    def peer(axis, k):
        index, size = here[axis]
        return {axis: lax.rem(index + k, size)}

    def remote(src, dst, send, recv, axis, k):
        return pltpu.make_async_remote_copy(
            src_ref=src, dst_ref=dst, send_sem=send, recv_sem=recv,
            device_id=peer(axis, k), device_id_type=MESH,
        )

    def lanes(h, width):
        return pl.ds(pl.multiple_of(h * width, width), width)

    def landed(view, sem):
        pltpu.make_async_copy(view, view, sem).wait()

    load_trunk = pltpu.make_async_copy(trunk_hbm, trunk, load_sem.at[0])
    load_branch = pltpu.make_async_copy(branch_hbm, branch, load_sem.at[1])

    def load_kv(h):
        pltpu.make_async_copy(wk_hbm.at[:, lanes(h, DH)], kw.at[h, ty, tx, tc], load_sem.at[2]).start()
        pltpu.make_async_copy(wv_hbm.at[:, lanes(h, DH)], vw.at[h, ty, tx, tc], load_sem.at[2]).start()

    def load_qo(p):
        pltpu.make_async_copy(wq_hbm.at[:, lanes(p, 256)], qw.at[p, ty, tx, tc], load_sem.at[3]).start()
        pltpu.make_async_copy(wo_hbm.at[:, lanes(p, 256)], ow.at[p, ty, tx, tc], load_sem.at[3]).start()

    def ways(first, second, s, r1, r2, r3):
        def one(g):
            for k in (2, 1, 3):
                a, b = first.at[g, ty, tx, tc], second.at[g, ty, tx, tc]
                remote(a, a, send.at[s], r1.at[g], "tx", k).start()
                remote(b, b, send.at[s], r1.at[g], "ty", k).start()

        def two(g):
            landed(first.at[0, 0, pl.ds(0, 3)], r1.at[g])
            for k in (2, 1, 3):
                a, b = first.at[g, ty, :, tc], second.at[g, :, tx, tc]
                remote(a, a, send.at[s + 1], r2.at[g], "ty", k).start()
                remote(b, b, send.at[s + 1], r2.at[g], "tx", k).start()

        def three(g):
            landed(first.at[0, pl.ds(0, 3)], r2.at[g])
            a, b = first.at[g, :, :, tc], second.at[g, :, :, tc]
            remote(a, a, send.at[s + 2], r3.at[g], "tc", 1).start()
            remote(b, b, send.at[s + 2], r3.at[g], "tc", 1).start()

        def ready(g):
            landed(first.at[0], r3.at[g])

        return one, two, three, ready

    kv_first, kv_second, kv_third, kv_ready = ways(kw, vw, 0, w1r, w2r, w3r)
    qo_first, qo_second, qo_third, qo_ready = ways(qw, ow, 3, u1r, u2r, u3r)

    def send_tot(h):
        remote(tot.at[h, 1 - tc], crecv.at[h], send.at[6], cr.at[lax.rem(h, 2)], "tc", 1).start()

    def send_x(h):
        for k in (2, 1, 3):
            remote(xsend.at[h], xrecv.at[h, k - 1], send.at[7], xr.at[lax.rem(h, 2)], "tx", k).start()

    def send_y(h):
        for k in (2, 1, 3):
            remote(ysend.at[h], yrecv.at[h, k - 1], send.at[8], yr.at[lax.rem(h, 2)], "ty", k).start()

    def send_p(h):
        remote(psend.at[h], carried.at[h, 1], send.at[9], pr.at[lax.rem(h, 2)], "tc", 1).start()

    def send_z(h, k):
        remote(sbuf.at[h, k], sv.at[h, leaf, pl.ds(0, DH)], send.at[10], zr.at[h], "leaf", k).start()

    barrier = pltpu.get_barrier_semaphore()
    partners = [("tc", 1), ("leaf", 1), ("leaf", LEAF - 1)]
    partners += [(axis, k) for axis in ("tx", "ty") for k in range(1, ROW)]
    for axis, k in partners:
        pl.semaphore_signal(barrier, inc=1, device_id=peer(axis, k), device_id_type=MESH)

    def vouch(i):
        for k in (1, LEAF - 1):
            pl.semaphore_signal(near.at[i], inc=1, device_id=peer("leaf", k), device_id_type=MESH)

    @pl.loop(0, H)
    def _(h):
        load_kv(h)

    load_trunk.start()
    load_branch.start()

    @pl.loop(0, 4)
    def _(p):
        load_qo(p)

    pl.semaphore_wait(barrier, len(partners))
    landed(kw.at[0, pl.ds(0, 2)], load_sem.at[2])
    kv_first(0)
    vouch(0)
    kv_second(0)

    @pl.loop(1, 4)
    def _(h):
        kv_first(h)

    kv_third(0)
    kv_second(1)
    kv_second(2)

    @pl.loop(4, H)
    def _(h):
        kv_first(h)

    load_trunk.wait()
    load_branch.wait()
    landed(qw.at[0, 0], load_sem.at[3])

    def weights(h):
        return jnp.concatenate([kw[h].reshape(1024, DH), vw[h].reshape(1024, DH)], axis=1)

    def flag(cond):
        return jnp.where(cond, 1.0, 0.0).astype(F32)

    def stage1(h):
        kv_ready(h)
        both = dot(trunk[...], weights(h))
        for r in range(2):
            part = both[r * 256 : (r + 1) * 256]
            value = part[:, DH:].astype(BF)
            turned = part[:, :DH].T.astype(BF)
            key_t[h, r] = turned
            val[h, r] = value
            tot[h, r] = dot(turned, value)
        send_tot(h)

    def stage2(h):
        landed(crecv.at[h], cr.at[lax.rem(h, 2)])
        xsend[h] = (tot[h, tc] + crecv[h]).astype(BF)
        send_x(h)

    def stage3(h):
        landed(xrecv.at[h], xr.at[lax.rem(h, 2)])
        row = tot[h, tc] + crecv[h]
        for k in range(ROW - 1):
            row = row + xrecv[h, k].astype(F32)
        ysend[h] = row.astype(BF)
        send_y(h)

    def stage4(h):
        landed(yrecv.at[h], yr.at[lax.rem(h, 2)])
        before = jnp.zeros((DH, DH), F32)
        for k in range(1, ROW):
            before = before + flag(ty >= k) * yrecv[h, k - 1].astype(F32)
            before = before + flag(tx >= k) * xrecv[h, k - 1].astype(F32)
        psend[h] = before + flag(tc == 0) * tot[h, tc]
        send_p(h)
        carried[h, 0] = before + flag(tc == 1) * crecv[h]

    shifts = (4, 3, 5, 2, 6, 1, 7, 0)

    def stage5(h):
        landed(psend.at[h], pr.at[lax.rem(h, 2)])
        position = lax.broadcasted_iota(jnp.int32, (DH, 256), 1)
        for k in shifts:
            lane = lax.rem(leaf + k, LEAF)
            tree = which[lane]
            kept = jnp.where(position < offset[lane], key_t[h, tree].astype(F32), 0.0).astype(BF)
            base = jnp.where(tree == tc, carried[h, 0], carried[h, 1])
            state = (base + dot(kept, val[h, tree])).astype(BF)
            if k == 0:
                sv[h, leaf, pl.ds(0, DH), :] = state
            else:
                sbuf[h, k] = state
        for k in shifts[:-1]:
            send_z(h, k)

    def branch_kv(h):
        both = dot(branch[...], weights(h)).astype(BF)
        for s in range(LEAF):
            part = both[s * DH : (s + 1) * DH]
            kb[h, s] = part[:, :DH]
            sv[h, s, pl.ds(DH, DH), :] = part[:, DH:]

    rows = lax.broadcasted_iota(jnp.int32, (DH, DH), 0)
    columns = lax.broadcasted_iota(jnp.int32, (DH, DH), 1)

    def branch_q(p):
        qo_ready(p)
        both = dot(branch[...], qw[p].reshape(1024, 256)).astype(BF)
        for s in range(LEAF):
            for u in range(2):
                query = both[s * DH : (s + 1) * DH, u * DH : (u + 1) * DH]
                scores = lax.dot_general(
                    query, kb[2 * p + u, s], (((1,), (1,)), ((), ())), preferred_element_type=F32
                )
                qwb[2 * p + u, s, :, pl.ds(0, DH)] = query
                qwb[2 * p + u, s, :, pl.ds(DH, DH)] = jnp.where(columns <= rows, scores, 0.0).astype(BF)

    @pl.loop(0, H + 4)
    def _(j):
        @pl.when(j < H)
        def _():
            stage1(j)

        @pl.when((j >= 2) & (j < H + 2))
        def _():
            stage4(j - 2)

        @pl.when((j >= 1) & (j < H + 1))
        def _():
            stage3(j - 1)

        @pl.when(j < H)
        def _():
            stage2(j)

        @pl.when(j == 0)
        def _():
            pl.semaphore_wait(near.at[0], 2)
            vouch(1)

        @pl.when(j == 1)
        def _():
            pl.semaphore_wait(near.at[1], 2)
            vouch(2)

        @pl.when(j == 2)
        def _():
            pl.semaphore_wait(near.at[2], 2)

        @pl.when(j >= 8)
        def _():
            branch_q(j - 8)

        @pl.when((j >= 2) & (j < H + 2))
        def _():
            stage5(j - 2)

        @pl.when(j + 1 < H)
        def _():
            kv_third(j + 1)

        @pl.when(j == 1)
        def _():
            kv_second(3)

        @pl.when((j >= 2) & (j < 4))
        def _():
            kv_second(2 * j)
            kv_second(2 * j + 1)

        @pl.when((j >= 3) & (j < 7))
        def _():
            qo_first(j - 3)

        @pl.when((j >= 5) & (j < 9))
        def _():
            qo_second(j - 5)

        @pl.when((j >= 7) & (j < 11))
        def _():
            qo_third(j - 7)

        @pl.when(j < H)
        def _():
            branch_kv(j)

    def finish(p):
        for u in range(2):
            h = 2 * p + u
            landed(sbuf.at[h, pl.ds(0, LEAF - 1)], zr.at[h])
            for s in range(LEAF):
                numerator = dot(qwb[h, s], sv[h, s])
                meansq = jnp.mean(numerator * numerator, axis=-1, keepdims=True)
                normed[s * DH : (s + 1) * DH, u * DH : (u + 1) * DH] = (
                    numerator * lax.rsqrt(meansq + 1e-06)
                ).astype(BF)

    def product(p, c):
        return dot(normed[...], ow[c, p].reshape(256, 256))

    landed(kw.at[pl.ds(0, 3), pl.ds(0, 2)], send.at[0])
    landed(kw.at[pl.ds(0, 6)], send.at[1])
    landed(kw, send.at[2])
    landed(qw.at[0, pl.ds(0, 3)], send.at[3])
    landed(qw.at[pl.ds(0, 3)], send.at[4])
    landed(qw, send.at[5])
    landed(crecv, send.at[6])
    landed(xrecv, send.at[7])
    landed(yrecv, send.at[8])
    landed(psend, send.at[9])

    finish(0)
    for c in range(4):
        acc[c] = product(0, c)

    @pl.loop(1, 3)
    def _(p):
        finish(p)
        for c in range(4):
            acc[c] += product(p, c)

    finish(3)
    place = lax.broadcasted_iota(jnp.int32, (DH, 256), 0)
    for c in range(4):
        total = acc[c] + product(3, c)
        for s in range(LEAF):
            result[s, :, c * 256 : (c + 1) * 256] = jnp.where(
                place < length[s], total[s * DH : (s + 1) * DH], 0.0
            ).astype(BF)

    landed(sbuf.at[pl.ds(0, LEAF - 1)], send.at[10])


def shards(
    trunk_tokens, branch_tokens, fork_offset, fork_tree, branch_len, w_query, w_key, w_value, w_out
):
    slots, blen, width = branch_tokens.shape
    dma = pltpu.SemaphoreType.DMA
    anywhere = pl.BlockSpec(memory_space=pltpu.HBM)
    small = pl.BlockSpec(memory_space=pltpu.SMEM)
    square = (DH, DH)
    vm = pltpu.VMEM
    return pl.pallas_call(
        kernel,
        out_shape=pltpu.VMEM((slots, blen, width), BF),
        in_specs=[anywhere, anywhere, small, small, small] + [anywhere] * 4,
        out_specs=pl.BlockSpec(memory_space=pltpu.VMEM),
        scratch_shapes=[
            vm((512, 1024), BF),
            vm((1024, 1024), BF),
            vm((H, ROW, ROW, 2, 32, DH), BF),
            vm((H, ROW, ROW, 2, 32, DH), BF),
            vm((4, ROW, ROW, 2, 32, 256), BF),
            vm((4, ROW, ROW, 2, 32, 256), BF),
            vm((H, 2, DH, 256), BF),
            vm((H, 2, 256, DH), BF),
            vm((H, 2) + square, F32),
            vm((H,) + square, F32),
            vm((H,) + square, BF),
            vm((H, ROW - 1) + square, BF),
            vm((H,) + square, BF),
            vm((H, ROW - 1) + square, BF),
            vm((H, 2) + square, F32),
            vm((H,) + square, F32),
            vm((H, LEAF) + square, BF),
            vm((H, LEAF, 256, DH), BF),
            vm((H, LEAF) + square, BF),
            vm((H, LEAF, DH, 256), BF),
            vm((1024, 256), BF),
            vm((4, 1024, 256), F32),
            dma((4,)),
            dma((H,)), dma((H,)), dma((H,)), dma((4,)), dma((4,)), dma((4,)),
            dma((2,)), dma((2,)), dma((2,)), dma((2,)), dma((H,)),
            dma((11,)), pltpu.SemaphoreType.REGULAR((3,)),
        ],
        compiler_params=pltpu.CompilerParams(
            collective_id=0, has_side_effects=True, vmem_limit_bytes=60 << 20
        ),
    )(
        trunk_tokens.reshape(-1, width), branch_tokens.reshape(-1, width),
        fork_offset.reshape(-1), fork_tree.reshape(-1), branch_len,
        w_query, w_key, w_value, w_out,
    )


def solution(mesh):
    split = Mesh(mesh.devices.reshape(LEAF, ROW, ROW, 2), AXES)
    return jax.shard_map(
        shards,
        mesh=split,
        in_specs=(
            P("leaf", TRUNK, None),
            P(AXES, None, None),
            P("leaf", TRUNK, None),
            P("leaf", TRUNK, None),
            P(AXES),
            P(TRUNK, None),
            P(TRUNK, None),
            P(TRUNK, None),
            P(TRUNK, None),
        ),
        out_specs=P(AXES, None, None),
        check_vma=False,
    )
```

```python
import jax
import jax.numpy as jnp
from jax import lax
from jax.experimental import pallas as pl
from jax.experimental.pallas import tpu as pltpu
from jax.sharding import Mesh
from jax.sharding import PartitionSpec as P

AXES = ("leaf", "ty", "tx", "tc")
TRUNK = AXES[1:]
MESH = pl.DeviceIdType.MESH
BF = jnp.bfloat16
F32 = jnp.float32
H = 8
DH = 128
LEAF = 8
ROW = 4


def dot(left, right):
    return jnp.dot(left, right, preferred_element_type=F32)


def kernel(
    trunk_hbm, branch_hbm, offset, which, length, wq_hbm, wk_hbm, wv_hbm, wo_hbm,
    result,
    trunk, branch, kw, vw, qw, ow, key_t, val, tot, crecv, xsend, xrecv, ysend, yrecv,
    carried, psend, sbuf, sv, kb, qwb, normed, acc,
    load_sem, w1r, w2r, w3r, u1r, u2r, u3r, cr, xr, yr, pr, zr, send, near,
):
    leaf = lax.axis_index("leaf")
    ty = lax.axis_index("ty")
    tx = lax.axis_index("tx")
    tc = lax.axis_index("tc")
    here = {"leaf": (leaf, LEAF), "ty": (ty, ROW), "tx": (tx, ROW), "tc": (tc, 2)}

    def peer(axis, k):
        index, size = here[axis]
        return {axis: lax.rem(index + k, size)}

    def remote(src, dst, send, recv, axis, k):
        return pltpu.make_async_remote_copy(
            src_ref=src, dst_ref=dst, send_sem=send, recv_sem=recv,
            device_id=peer(axis, k), device_id_type=MESH,
        )

    def lanes(h, width):
        return pl.ds(pl.multiple_of(h * width, width), width)

    def landed(view, sem):
        pltpu.make_async_copy(view, view, sem).wait()

    load_trunk = pltpu.make_async_copy(trunk_hbm, trunk, load_sem.at[0])
    load_branch = pltpu.make_async_copy(branch_hbm, branch, load_sem.at[1])

    def load_kv(h):
        pltpu.make_async_copy(wk_hbm.at[:, lanes(h, DH)], kw.at[h, ty, tx, tc], load_sem.at[2]).start()
        pltpu.make_async_copy(wv_hbm.at[:, lanes(h, DH)], vw.at[h, ty, tx, tc], load_sem.at[2]).start()

    def load_qo(p):
        pltpu.make_async_copy(wq_hbm.at[:, lanes(p, 256)], qw.at[p, ty, tx, tc], load_sem.at[3]).start()
        pltpu.make_async_copy(wo_hbm.at[:, lanes(p, 256)], ow.at[p, ty, tx, tc], load_sem.at[3]).start()

    def ways(first, second, s, r1, r2, r3):
        def one(g):
            for k in (2, 1, 3):
                a, b = first.at[g, ty, tx, tc], second.at[g, ty, tx, tc]
                remote(a, a, send.at[s], r1.at[g], "tx", k).start()
                remote(b, b, send.at[s], r1.at[g], "ty", k).start()

        def two(g):
            landed(first.at[0, 0, pl.ds(0, 3)], r1.at[g])
            for k in (2, 1, 3):
                a, b = first.at[g, ty, :, tc], second.at[g, :, tx, tc]
                remote(a, a, send.at[s + 1], r2.at[g], "ty", k).start()
                remote(b, b, send.at[s + 1], r2.at[g], "tx", k).start()

        def three(g):
            landed(first.at[0, pl.ds(0, 3)], r2.at[g])
            a, b = first.at[g, :, :, tc], second.at[g, :, :, tc]
            remote(a, a, send.at[s + 2], r3.at[lax.rem(g, 2)], "tc", 1).start()
            remote(b, b, send.at[s + 2], r3.at[lax.rem(g, 2)], "tc", 1).start()

        def ready(g):
            landed(first.at[0], r3.at[lax.rem(g, 2)])

        return one, two, three, ready

    kv_first, kv_second, kv_third, kv_ready = ways(kw, vw, 0, w1r, w2r, w3r)
    qo_first, qo_second, qo_third, qo_ready = ways(qw, ow, 3, u1r, u2r, u3r)

    def send_tot(h):
        remote(tot.at[h, 1 - tc], crecv.at[h], send.at[6], cr.at[lax.rem(h, 2)], "tc", 1).start()

    def send_x(h):
        for k in (2, 1, 3):
            remote(xsend.at[h], xrecv.at[h, k - 1], send.at[7], xr.at[lax.rem(h, 2)], "tx", k).start()

    def send_y(h):
        for k in (2, 1, 3):
            remote(ysend.at[h], yrecv.at[h, k - 1], send.at[8], yr.at[lax.rem(h, 2)], "ty", k).start()

    def send_p(h):
        remote(psend.at[h], carried.at[h, 1], send.at[9], pr.at[lax.rem(h, 2)], "tc", 1).start()

    def send_z(h, k):
        remote(sbuf.at[h, k], sv.at[h, leaf, pl.ds(0, DH)], send.at[10], zr.at[h], "leaf", k).start()

    barrier = pltpu.get_barrier_semaphore()
    partners = [("tc", 1), ("leaf", 1), ("leaf", LEAF - 1)]
    partners += [(axis, k) for axis in ("tx", "ty") for k in range(1, ROW)]
    for axis, k in partners:
        pl.semaphore_signal(barrier, inc=1, device_id=peer(axis, k), device_id_type=MESH)

    def vouch(i):
        for k in (1, LEAF - 1):
            pl.semaphore_signal(near.at[i], inc=1, device_id=peer("leaf", k), device_id_type=MESH)

    @pl.loop(0, H)
    def _(h):
        load_kv(h)

    load_trunk.start()
    load_branch.start()

    @pl.loop(0, 4)
    def _(p):
        load_qo(p)

    pl.semaphore_wait(barrier, len(partners))
    landed(kw.at[0, pl.ds(0, 2)], load_sem.at[2])
    kv_first(0)
    vouch(0)
    kv_second(0)

    @pl.loop(1, 4)
    def _(h):
        kv_first(h)

    kv_third(0)
    kv_second(1)
    kv_second(2)

    @pl.loop(4, H)
    def _(h):
        kv_first(h)

    load_trunk.wait()
    load_branch.wait()
    landed(qw.at[0, 0], load_sem.at[3])

    def weights(h):
        return jnp.concatenate([kw[h].reshape(1024, DH), vw[h].reshape(1024, DH)], axis=1)

    def flag(cond):
        return jnp.where(cond, 1.0, 0.0).astype(F32)

    def stage1(h):
        kv_ready(h)
        both = dot(trunk[...], weights(h))
        for r in range(2):
            part = both[r * 256 : (r + 1) * 256]
            value = part[:, DH:].astype(BF)
            turned = part[:, :DH].T.astype(BF)
            key_t[h, r] = turned
            val[h, r] = value
            tot[h, r] = dot(turned, value)
        send_tot(h)

    def stage2(h):
        landed(crecv.at[h], cr.at[lax.rem(h, 2)])
        xsend[h] = (tot[h, tc] + crecv[h]).astype(BF)
        send_x(h)

    def stage3(h):
        landed(xrecv.at[h], xr.at[lax.rem(h, 2)])
        row = tot[h, tc] + crecv[h]
        for k in range(ROW - 1):
            row = row + xrecv[h, k].astype(F32)
        ysend[h] = row.astype(BF)
        send_y(h)

    def stage4(h):
        landed(yrecv.at[h], yr.at[lax.rem(h, 2)])
        before = jnp.zeros((DH, DH), F32)
        for k in range(1, ROW):
            before = before + flag(ty >= k) * yrecv[h, k - 1].astype(F32)
            before = before + flag(tx >= k) * xrecv[h, k - 1].astype(F32)
        psend[h] = before + flag(tc == 0) * tot[h, tc]
        send_p(h)
        carried[h, 0] = before + flag(tc == 1) * crecv[h]

    shifts = (4, 3, 5, 2, 6, 1, 7, 0)

    def stage5(h):
        landed(psend.at[h], pr.at[lax.rem(h, 2)])
        position = lax.broadcasted_iota(jnp.int32, (DH, 256), 1)
        for k in shifts:
            lane = lax.rem(leaf + k, LEAF)
            tree = which[lane]
            kept = jnp.where(position < offset[lane], key_t[h, tree].astype(F32), 0.0).astype(BF)
            base = jnp.where(tree == tc, carried[h, 0], carried[h, 1])
            state = (base + dot(kept, val[h, tree])).astype(BF)
            if k == 0:
                sv[h, leaf, pl.ds(0, DH), :] = state
            else:
                sbuf[h, k] = state
        for k in shifts[:-1]:
            send_z(h, k)

    def branch_kv(h):
        both = dot(branch[...], weights(h)).astype(BF)
        for s in range(LEAF):
            part = both[s * DH : (s + 1) * DH]
            kb[h, s] = part[:, :DH]
            sv[h, s, pl.ds(DH, DH), :] = part[:, DH:]

    rows = lax.broadcasted_iota(jnp.int32, (DH, DH), 0)
    columns = lax.broadcasted_iota(jnp.int32, (DH, DH), 1)

    def branch_q(p):
        qo_ready(p)
        both = dot(branch[...], qw[p].reshape(1024, 256)).astype(BF)
        for s in range(LEAF):
            for u in range(2):
                query = both[s * DH : (s + 1) * DH, u * DH : (u + 1) * DH]
                scores = lax.dot_general(
                    query, kb[2 * p + u, s], (((1,), (1,)), ((), ())), preferred_element_type=F32
                )
                qwb[2 * p + u, s, :, pl.ds(0, DH)] = query
                qwb[2 * p + u, s, :, pl.ds(DH, DH)] = jnp.where(columns <= rows, scores, 0.0).astype(BF)

    @pl.loop(0, H + 4)
    def _(j):
        @pl.when(j < H)
        def _():
            stage1(j)

        @pl.when((j >= 2) & (j < H + 2))
        def _():
            stage4(j - 2)

        @pl.when((j >= 1) & (j < H + 1))
        def _():
            stage3(j - 1)

        @pl.when(j < H)
        def _():
            stage2(j)

        @pl.when(j == 0)
        def _():
            pl.semaphore_wait(near.at[0], 2)
            vouch(1)

        @pl.when(j == 1)
        def _():
            pl.semaphore_wait(near.at[1], 2)
            vouch(2)

        @pl.when(j == 2)
        def _():
            pl.semaphore_wait(near.at[2], 2)

        @pl.when(j >= 8)
        def _():
            branch_q(j - 8)

        @pl.when((j >= 2) & (j < H + 2))
        def _():
            stage5(j - 2)

        @pl.when(j + 1 < H)
        def _():
            kv_third(j + 1)

        @pl.when(j == 1)
        def _():
            kv_second(3)

        @pl.when((j >= 2) & (j < 4))
        def _():
            kv_second(2 * j)
            kv_second(2 * j + 1)

        @pl.when((j >= 3) & (j < 7))
        def _():
            qo_first(j - 3)

        @pl.when((j >= 5) & (j < 9))
        def _():
            qo_second(j - 5)

        @pl.when((j >= 7) & (j < 11))
        def _():
            qo_third(j - 7)

        @pl.when(j < H)
        def _():
            branch_kv(j)

    def finish(p):
        for u in range(2):
            h = 2 * p + u
            landed(sbuf.at[h, pl.ds(0, LEAF - 1)], zr.at[h])
            for s in range(LEAF):
                numerator = dot(qwb[h, s], sv[h, s])
                meansq = jnp.mean(numerator * numerator, axis=-1, keepdims=True)
                normed[s * DH : (s + 1) * DH, u * DH : (u + 1) * DH] = (
                    numerator * lax.rsqrt(meansq + 1e-06)
                ).astype(BF)

    def product(p, c):
        return dot(normed[...], ow[c, p].reshape(256, 256))

    landed(kw.at[pl.ds(0, 3), pl.ds(0, 2)], send.at[0])
    landed(kw.at[pl.ds(0, 6)], send.at[1])
    landed(kw, send.at[2])
    landed(qw.at[0, pl.ds(0, 3)], send.at[3])
    landed(qw.at[pl.ds(0, 3)], send.at[4])
    landed(qw, send.at[5])
    landed(crecv, send.at[6])
    landed(xrecv, send.at[7])
    landed(yrecv, send.at[8])
    landed(psend, send.at[9])

    finish(0)
    for c in range(4):
        acc[c] = product(0, c)

    @pl.loop(1, 3)
    def _(p):
        finish(p)
        for c in range(4):
            acc[c] += product(p, c)

    finish(3)
    place = lax.broadcasted_iota(jnp.int32, (DH, 256), 0)
    for c in range(4):
        total = acc[c] + product(3, c)
        for s in range(LEAF):
            result[s, :, c * 256 : (c + 1) * 256] = jnp.where(
                place < length[s], total[s * DH : (s + 1) * DH], 0.0
            ).astype(BF)

    landed(sbuf.at[pl.ds(0, LEAF - 1)], send.at[10])


def shards(
    trunk_tokens, branch_tokens, fork_offset, fork_tree, branch_len, w_query, w_key, w_value, w_out
):
    slots, blen, width = branch_tokens.shape
    dma = pltpu.SemaphoreType.DMA
    anywhere = pl.BlockSpec(memory_space=pltpu.HBM)
    small = pl.BlockSpec(memory_space=pltpu.SMEM)
    square = (DH, DH)
    vm = pltpu.VMEM
    return pl.pallas_call(
        kernel,
        out_shape=pltpu.VMEM((slots, blen, width), BF),
        in_specs=[anywhere, anywhere, small, small, small] + [anywhere] * 4,
        out_specs=pl.BlockSpec(memory_space=pltpu.VMEM),
        scratch_shapes=[
            vm((512, 1024), BF),
            vm((1024, 1024), BF),
            vm((H, ROW, ROW, 2, 32, DH), BF),
            vm((H, ROW, ROW, 2, 32, DH), BF),
            vm((4, ROW, ROW, 2, 32, 256), BF),
            vm((4, ROW, ROW, 2, 32, 256), BF),
            vm((H, 2, DH, 256), BF),
            vm((H, 2, 256, DH), BF),
            vm((H, 2) + square, F32),
            vm((H,) + square, F32),
            vm((H,) + square, BF),
            vm((H, ROW - 1) + square, BF),
            vm((H,) + square, BF),
            vm((H, ROW - 1) + square, BF),
            vm((H, 2) + square, F32),
            vm((H,) + square, F32),
            vm((H, LEAF) + square, BF),
            vm((H, LEAF, 256, DH), BF),
            vm((H, LEAF) + square, BF),
            vm((H, LEAF, DH, 256), BF),
            vm((1024, 256), BF),
            vm((4, 1024, 256), F32),
            dma((4,)),
            dma((H,)), dma((H,)), dma((2,)), dma((4,)), dma((4,)), dma((2,)),
            dma((2,)), dma((2,)), dma((2,)), dma((2,)), dma((H,)),
            dma((11,)), pltpu.SemaphoreType.REGULAR((3,)),
        ],
        compiler_params=pltpu.CompilerParams(
            collective_id=0, has_side_effects=True, vmem_limit_bytes=60 << 20
        ),
    )(
        trunk_tokens.reshape(-1, width), branch_tokens.reshape(-1, width),
        fork_offset.reshape(-1), fork_tree.reshape(-1), branch_len,
        w_query, w_key, w_value, w_out,
    )


def solution(mesh):
    split = Mesh(mesh.devices.reshape(LEAF, ROW, ROW, 2), AXES)
    return jax.shard_map(
        shards,
        mesh=split,
        in_specs=(
            P("leaf", TRUNK, None),
            P(AXES, None, None),
            P("leaf", TRUNK, None),
            P("leaf", TRUNK, None),
            P(AXES),
            P(TRUNK, None),
            P(TRUNK, None),
            P(TRUNK, None),
            P(TRUNK, None),
        ),
        out_specs=P(AXES, None, None),
        check_vma=False,
    )
```
